32 devices in a mesh: groups: 2 (over x), win: 4 (over y, core), rcv: 4 (over z).
Axes of the slice: x: 2, y: 2, z: 4, core: 2. Of those that a mesh axis runs over, the one named last changes fastest.
Arguments:
- traces: bfloat16 [32, 768, 4096], P('win', ('groups', 'rcv')), parts along dimension 1, may hold values from -6 to 6
- valid: int32 [64], P(('groups', 'win')), parts along dimension 0, may hold values 0 or 1
- src_station: int32 [64], P('groups'), parts along dimension 0, may hold values from 0 to 383, as said below
Outputs:
- stacks: float32 [32, 768, 2, 512], P(None, ('groups', 'rcv'), None, 'win'), parts along dimension 1
The draws below stay inside these ranges and needn't reach their ends.
There are 2 independent parts, one for each index of `groups`. The reference program is written for one: setup_inputs(seed, part) draws one part's arguments, and reference() takes and returns one part's arrays. A program takes and returns all parts, laid end to end along the dimension named above; each array names one. Nothing has to cross between parts.
Inputs may be any that keep to these rules, and one draw needn't show every extreme that they name: `src_station`: distinct stations; station 0 and station 384 - 1 are always among them.
All inputs are finite; a program needn't handle non-finite values. No bound on the sum of `valid` on one device may be relied on, other than what follows from the above.
Results may differ from the reference program's by a relative error of at most 0.0049.
Values may be sent and summed in bfloat16 or wider, within the bound.
A program may use at most 128 MiB of HBM per device.

```python
import math
import jax
import jax.numpy as jnp
from jax import lax

NT = 4096
F = 512
K0 = 256
SOURCES = 32
WINDOWS = 32
RECEIVERS = 384


def draw_src_station(key, part):
    inner = jax.random.permutation(key, RECEIVERS - 2)[:SOURCES - 2].astype(jnp.int32) + 1
    ends = jnp.array([0, RECEIVERS - 1], dtype=jnp.int32)
    picked = jnp.concatenate([ends, inner])
    return jax.random.permutation(jax.random.fold_in(key, 7), picked).astype(jnp.int32)


def place_ends(entries, rng, smallest, top_value):
    place = [jax.random.randint(jax.random.fold_in(rng, axis), (), 0, length) for axis, length in enumerate(entries.shape)]
    longest = entries.shape.index(max(entries.shape))
    beside = place[:longest] + [(place[longest] + 1) % entries.shape[longest]] + place[longest + 1:]
    return entries.at[tuple(place)].set(smallest).at[tuple(beside)].set(top_value)


def block_levels(key, dims, pieces, least, largest):
    def one(dim, shards_of):
        draws = jax.random.uniform(jax.random.fold_in(jax.random.fold_in(key, 6), dim), (shards_of,), jnp.float32, least / len(pieces), largest / len(pieces))
        return jnp.repeat(jnp.exp(draws), dims[dim] // shards_of).reshape((-1,) + (1,) * (len(dims) - dim - 1))

    factor_of = one(*pieces[0])
    for cut in pieces[1:]:
        factor_of = factor_of * one(*cut)
    return factor_of


def scatter_about(rng, dims, scale, bound, shards=(), kind=jnp.bfloat16):
    level = block_levels(rng, dims, shards, -0.22, 0.18) if shards else 1.0
    entries = jax.random.normal(rng, dims, jnp.float32) * scale * level
    return jnp.minimum(jnp.maximum(entries, -bound), bound).astype(kind)


def setup_inputs(seed: int = 0, part: int = 0) -> dict:
    key_of = jax.random.split(jax.random.key(seed), 4)
    own_keys = jax.random.split(jax.random.fold_in(key_of[3], part), 4)
    traces = scatter_about(own_keys[0], (WINDOWS, RECEIVERS, NT), 1.0, 6.0, ((0, 4), (1, 4)))
    valid = place_ends((jax.random.randint(own_keys[1], (WINDOWS,), 0, 4) < 3).astype(jnp.int32), jax.random.fold_in(own_keys[1], 1), 0, 1)
    src_station = draw_src_station(jax.random.fold_in(jax.random.fold_in(key_of[3], part), 71), part)
    return dict(traces=traces, valid=valid, src_station=src_station)


def band_table(count, bins, first):
    samples = jnp.arange(count, dtype=jnp.int32)
    freqs = first + jnp.arange(bins, dtype=jnp.int32)
    phase = samples[:, None] * freqs[None, :] % count
    angle = phase.astype(jnp.float32) * (2.0 * math.pi / count)
    return jnp.concatenate([jnp.cos(angle), -jnp.sin(angle)], axis=1).astype(jnp.bfloat16)

def reference(traces, valid, src_station):
    table = band_table(NT, F, K0)

    def whiten(window):
        spectra = jnp.dot(window, table, preferred_element_type=jnp.float32)
        spectra = spectra.reshape(window.shape[0], 2, F)
        power = lax.optimization_barrier(jnp.sum(spectra * spectra, axis=(1, 2), keepdims=True)) / F
        return (spectra * lax.rsqrt(power + 1e-06)).astype(jnp.bfloat16)
    white = lax.map(whiten, traces)
    received = white * valid.astype(jnp.bfloat16)[:, None, None, None]
    sources = white[:, src_station]
    rr = received[:, :, 0].astype(jnp.float32)
    ri = received[:, :, 1].astype(jnp.float32)
    sr = sources[:, :, 0].astype(jnp.float32)
    si = sources[:, :, 1].astype(jnp.float32)
    real = jnp.einsum('wsf,wrf->srf', sr, rr) + jnp.einsum('wsf,wrf->srf', si, ri)
    imag = jnp.einsum('wsf,wrf->srf', sr, ri) - jnp.einsum('wsf,wrf->srf', si, rr)
    return jnp.stack([real, imag], axis=2) * (1.0 / math.sqrt(WINDOWS))
```

```python
import math

import jax
import jax.numpy as jnp
import ml_dtypes
import numpy as np
from jax import lax
from jax.sharding import PartitionSpec as P

F = 512


def band_table(count, bins, first):
    samples = np.arange(count, dtype=np.int64)
    freqs = first + np.arange(bins, dtype=np.int64)
    phase = samples[:, None] * freqs[None, :] % count
    angle = phase.astype(np.float64) * (2.0 * math.pi / count)
    return np.concatenate([np.cos(angle), -np.sin(angle)], axis=1).astype(ml_dtypes.bfloat16)


def body(traces, valid, src_station):
    w_dev, r_dev, samples = traces.shape
    bins = F
    n_win = lax.axis_size("win")
    f_dev = bins // n_win
    table = jnp.asarray(band_table(samples, bins, samples // 16))
    spectra = jnp.dot(
        traces.reshape(w_dev * r_dev, samples), table, preferred_element_type=jnp.float32
    )
    power = jnp.sum(spectra * spectra, axis=1, keepdims=True) / bins
    keep = jnp.repeat(valid.astype(jnp.float32), r_dev)[:, None]
    white = (spectra * (lax.rsqrt(power + 1e-06) * keep)).astype(jnp.bfloat16)
    white = white.reshape(w_dev * r_dev, 2, n_win, f_dev)
    pieces = jnp.transpose(white, (2, 1, 0, 3))
    got = lax.all_to_all(pieces, "win", 0, 0, tiled=True)
    got = got.reshape(n_win, 2, w_dev, r_dev, f_dev)
    offset = lax.axis_index("rcv") * r_dev
    station_ids = offset + jnp.arange(r_dev, dtype=jnp.int32)
    selector = (src_station[:, None] == station_ids[None, :]).astype(jnp.bfloat16)
    rows = jnp.einsum("sr,gcwrf->gcwsf", selector, got, preferred_element_type=jnp.float32)
    src = lax.psum(rows.astype(jnp.bfloat16), "rcv")
    scale = 1.0 / math.sqrt(w_dev * n_win)
    turned = jnp.stack([got[:, 1], -got[:, 0]], axis=1)
    real = jnp.einsum("gcwsf,gcwrf->srf", src, got, preferred_element_type=jnp.float32)
    imag = jnp.einsum("gcwsf,gcwrf->srf", src, turned, preferred_element_type=jnp.float32)
    return jnp.stack([real, imag], axis=2) * scale


def solution(mesh):
    return jax.shard_map(
        body,
        mesh=mesh,
        in_specs=(P("win", ("groups", "rcv"), None), P(("groups", "win")), P("groups")),
        out_specs=P(None, ("groups", "rcv"), None, "win"),
        check_vma=False,
    )
```

```python
import functools
import math

import jax
import jax.numpy as jnp
import ml_dtypes
import numpy as np
from jax import lax
from jax.experimental import pallas as pl
from jax.experimental.pallas import tpu as pltpu
from jax.sharding import PartitionSpec as P

F = 512
SPLIT = 64
MM = 2
MESH = pl.DeviceIdType.MESH


def band_table(count, bins, first):
    samples = np.arange(count, dtype=np.int64)
    freqs = first + np.arange(bins, dtype=np.int64)
    phase = samples[:, None] * freqs[None, :] % count
    angle = phase.astype(np.float64) * (2.0 * math.pi / count)
    return np.concatenate([np.cos(angle), -np.sin(angle)], axis=1).astype(ml_dtypes.bfloat16)


def angle_factors(count, bins, first):
    freqs = first + np.arange(bins, dtype=np.int64)
    coarse = np.arange(count // SPLIT, dtype=np.int64)[:, None] * SPLIT * freqs[None, :] % count
    fine = np.arange(SPLIT, dtype=np.int64)[:, None] * freqs[None, :] % count
    out = []
    for phase in (coarse, fine):
        angle = phase.astype(np.float64) * (2.0 * math.pi / count)
        out += [np.cos(angle).astype(np.float32), np.sin(angle).astype(np.float32)]
    return out


def plain_body(traces, valid, src_station):
    w_dev, r_dev, samples = traces.shape
    bins = F
    n_win = lax.axis_size("win")
    f_dev = bins // n_win
    table = jnp.asarray(band_table(samples, bins, samples // 16))
    spectra = jnp.dot(
        traces.reshape(w_dev * r_dev, samples), table, preferred_element_type=jnp.float32
    )
    power = jnp.sum(spectra * spectra, axis=1, keepdims=True) / bins
    keep = jnp.repeat(valid.astype(jnp.float32), r_dev)[:, None]
    white = (spectra * (lax.rsqrt(power + 1e-06) * keep)).astype(jnp.bfloat16)
    white = white.reshape(w_dev * r_dev, 2, n_win, f_dev)
    pieces = jnp.transpose(white, (2, 1, 0, 3))
    got = lax.all_to_all(pieces, "win", 0, 0, tiled=True)
    got = got.reshape(n_win, 2, w_dev, r_dev, f_dev)
    offset = lax.axis_index("rcv") * r_dev
    station_ids = offset + jnp.arange(r_dev, dtype=jnp.int32)
    selector = (src_station[:, None] == station_ids[None, :]).astype(jnp.bfloat16)
    rows = jnp.einsum("sr,gcwrf->gcwsf", selector, got, preferred_element_type=jnp.float32)
    src = lax.psum(rows.astype(jnp.bfloat16), "rcv")
    scale = 1.0 / math.sqrt(w_dev * n_win)
    turned = jnp.stack([got[:, 1], -got[:, 0]], axis=1)
    real = jnp.einsum("gcwsf,gcwrf->srf", src, got, preferred_element_type=jnp.float32)
    imag = jnp.einsum("gcwsf,gcwrf->srf", src, turned, preferred_element_type=jnp.float32)
    return jnp.stack([real, imag], axis=2) * scale


def kernel(
    nw, nz, w_dev, r_dev, bins,
    traces, c1, s1, c0, s0, keep, sel, out,
    tr, table, spec, snd, got, own, pin, sin, pout, sout, srcf, rf,
    tsem, ysend, yrecv, psend, precv, ssend, srecv,
):
    me = lax.axis_index("win")
    z = lax.axis_index("rcv")
    f_dev = bins // nw
    peers = [lax.rem(me + d, nw) for d in range(1, nw)]
    senders = [lax.rem(me + nw - d, nw) for d in range(1, nw)]
    barrier = pltpu.get_barrier_semaphore()

    def load(w):
        return pltpu.make_async_copy(traces.at[w], tr.at[w], tsem.at[w])

    for w in range(w_dev):
        load(w).start()
    for peer in peers:
        pl.semaphore_signal(barrier, inc=1, device_id={"win": peer}, device_id_type=MESH)

    @pl.when(z > 0)
    def _():
        pl.semaphore_signal(barrier, inc=1, device_id={"rcv": z - 1}, device_id_type=MESH)

    @pl.when(z < nz - 1)
    def _():
        pl.semaphore_signal(barrier, inc=1, device_id={"rcv": z + 1}, device_id_type=MESH)

    @pl.when(z == 0)
    def _():
        pin[...] = jnp.zeros_like(pin)

    @pl.when(z == nz - 1)
    def _():
        sin[...] = jnp.zeros_like(sin)

    def build(a, _):
        ca, sa = c1[pl.ds(a, 1), :], s1[pl.ds(a, 1), :]
        rows = pl.ds(pl.multiple_of(a * SPLIT, SPLIT), SPLIT)
        table[rows, 0:bins] = (ca * c0[...] - sa * s0[...]).astype(jnp.bfloat16)
        table[rows, bins:] = (-(sa * c0[...] + ca * s0[...])).astype(jnp.bfloat16)
        return 0

    lax.fori_loop(0, c1.shape[0], build, 0)
    out[...] = jnp.zeros_like(out)

    @pl.when((z > 0) & (z < nz - 1))
    def _():
        pl.semaphore_wait(barrier, nw + 1)

    @pl.when((z == 0) | (z == nz - 1))
    def _():
        pl.semaphore_wait(barrier, nw)

    def y_copy(k, w):
        return pltpu.make_async_remote_copy(
            src_ref=snd.at[peers[k], w], dst_ref=got.at[me, w],
            send_sem=ysend.at[k, w], recv_sem=yrecv.at[k, w],
            device_id={"win": peers[k]}, device_id_type=MESH,
        )

    def y_arrival(k, w):
        return pltpu.make_async_remote_copy(
            src_ref=snd.at[peers[k], w], dst_ref=got.at[senders[k], w],
            send_sem=ysend.at[k, w], recv_sem=yrecv.at[k, w],
            device_id={"win": peers[k]}, device_id_type=MESH,
        )

    def transform(t, _):
        for wl in range(MM):
            load(t * MM + wl).wait()
        x = tr[pl.ds(t * MM, MM)].reshape(MM * r_dev, tr.shape[2])
        for nb in range(2 * bins // 256):
            cols = slice(nb * 256, nb * 256 + 256)
            spec[:, cols] = jnp.dot(x, table[:, cols], preferred_element_type=jnp.float32)
        for wl in range(MM):
            w = t * MM + wl
            rows = slice(wl * r_dev, (wl + 1) * r_dev)
            s = spec[rows, :]
            power = jnp.sum(s * s, axis=1, keepdims=True) / bins
            gain = lax.rsqrt(power + 1e-06) * keep[w][:, 0:1]
            for d in range(nw):
                for c in range(2):
                    lo = c * bins + d * f_dev
                    snd[d, w, c] = (spec[rows, lo:lo + f_dev] * gain).astype(jnp.bfloat16)
            for k in range(nw - 1):
                y_copy(k, w).start()
            got[me, w] = snd[me, w]
        return 0

    lax.fori_loop(0, w_dev // MM, transform, 0)

    def right(j):
        return pltpu.make_async_remote_copy(
            src_ref=pout.at[j], dst_ref=pin.at[j], send_sem=psend.at[j], recv_sem=precv.at[j],
            device_id={"rcv": lax.rem(z + 1, nz)}, device_id_type=MESH,
        )

    def left(j):
        return pltpu.make_async_remote_copy(
            src_ref=sout.at[j], dst_ref=sin.at[j], send_sem=ssend.at[j], recv_sem=srecv.at[j],
            device_id={"rcv": lax.rem(z + nz - 1, nz)}, device_id_type=MESH,
        )

    def step(it, _):
        @pl.when(it < w_dev)
        def _():
            for k in range(nw - 1):
                y_arrival(k, it).wait_recv()
            for g in range(nw):
                for c in range(2):
                    own[it, g, c] = jnp.dot(
                        sel[...], got[g, it, c], preferred_element_type=jnp.float32
                    ).astype(jnp.bfloat16)

        jr = it - z

        @pl.when((jr >= 0) & (jr < w_dev))
        def _():
            @pl.when(z > 0)
            def _():
                right(jr).wait_recv()

            @pl.when(z < nz - 1)
            def _():
                pout[jr] = own[jr] + pin[jr]
                right(jr).start()

        jl = it - (nz - 1 - z)

        @pl.when((jl >= 0) & (jl < w_dev))
        def _():
            @pl.when(z < nz - 1)
            def _():
                left(jl).wait_recv()

            @pl.when(z > 0)
            def _():
                sout[jl] = own[jl] + sin[jl]
                left(jl).start()

        jc = it - (nz - 1)

        @pl.when(jc >= 0)
        def _():
            srcf[...] = (own[jc] + pin[jc] + sin[jc]).astype(jnp.float32)
            for g in range(nw):
                re = got[g, jc, 0].astype(jnp.float32)
                im = got[g, jc, 1].astype(jnp.float32)
                rf[g, 0, pl.ds(0, r_dev, stride=2), :] = re
                rf[g, 0, pl.ds(1, r_dev, stride=2), :] = im
                rf[g, 1, pl.ds(0, r_dev, stride=2), :] = im
                rf[g, 1, pl.ds(1, r_dev, stride=2), :] = -re

            def accumulate(s, _):
                total = out[s]
                for g in range(nw):
                    total = total + srcf[g, 0, pl.ds(s, 1), :] * rf[g, 0]
                    total = total + srcf[g, 1, pl.ds(s, 1), :] * rf[g, 1]
                out[s] = total
                return 0

            lax.fori_loop(0, out.shape[0], accumulate, 0)

        return 0

    lax.fori_loop(0, w_dev + nz - 1, step, 0)

    def drain(w, _):
        for k in range(nw - 1):
            y_copy(k, w).wait_send()

        @pl.when(z < nz - 1)
        def _():
            right(w).wait_send()

        @pl.when(z > 0)
        def _():
            left(w).wait_send()

        return 0

    lax.fori_loop(0, w_dev, drain, 0)


def body(traces, valid, src_station):
    w_dev, r_dev, samples = traces.shape
    nw, nz = lax.axis_size("win"), lax.axis_size("rcv")
    f_dev = F // nw
    n_src = src_station.shape[0]
    if f_dev % 128 or r_dev % 16 or w_dev % MM:
        return plain_body(traces, valid, src_station)
    factors = [jnp.asarray(f) for f in angle_factors(samples, F, samples // 16)]
    station_ids = lax.axis_index("rcv") * r_dev + jnp.arange(r_dev, dtype=jnp.int32)
    sel = (src_station[:, None] == station_ids[None, :]).astype(jnp.bfloat16)
    keep = jnp.broadcast_to(valid.astype(jnp.float32)[:, None, None], (w_dev, 1, 128))
    vmem = pl.BlockSpec(memory_space=pltpu.VMEM)
    bf16, f32 = jnp.bfloat16, jnp.float32
    spectra = (nw, w_dev, 2, r_dev, f_dev)
    rows = (w_dev, nw, 2, n_src, f_dev)
    dma = pltpu.SemaphoreType.DMA
    stacks = pl.pallas_call(
        functools.partial(kernel, nw, nz, w_dev, r_dev, F),
        out_shape=jax.ShapeDtypeStruct((n_src, 2 * r_dev, f_dev), f32),
        in_specs=[pl.BlockSpec(memory_space=pl.ANY)] + [vmem] * 6,
        out_specs=vmem,
        scratch_shapes=[
            pltpu.VMEM((w_dev, r_dev, samples), bf16),
            pltpu.VMEM((samples, 2 * F), bf16),
            pltpu.VMEM((MM * r_dev, 2 * F), f32),
            pltpu.VMEM(spectra, bf16),
            pltpu.VMEM(spectra, bf16),
        ] + [pltpu.VMEM(rows, bf16)] * 5 + [
            pltpu.VMEM((nw, 2, n_src, f_dev), f32),
            pltpu.VMEM((nw, 2, 2 * r_dev, f_dev), f32),
            dma((w_dev,)), dma((nw - 1, w_dev)), dma((nw - 1, w_dev)),
            dma((w_dev,)), dma((w_dev,)), dma((w_dev,)), dma((w_dev,)),
        ],
        compiler_params=pltpu.CompilerParams(
            collective_id=0, has_side_effects=True, vmem_limit_bytes=56 * 1024 * 1024
        ),
    )(traces, *factors, keep, sel)
    scale = 1.0 / math.sqrt(w_dev * nw)
    return (stacks * scale).reshape(n_src, r_dev, 2, f_dev)


def solution(mesh):
    return jax.shard_map(
        body,
        mesh=mesh,
        in_specs=(P("win", ("groups", "rcv"), None), P(("groups", "win")), P("groups")),
        out_specs=P(None, ("groups", "rcv"), None, "win"),
        check_vma=False,
    )
```

```python
import functools
import math

import jax
import jax.numpy as jnp
import ml_dtypes
import numpy as np
from jax import lax
from jax.experimental import pallas as pl
from jax.experimental.pallas import tpu as pltpu
from jax.sharding import PartitionSpec as P

F = 512
SPLIT = 64
MM = 2
LAG = 1
MESH = pl.DeviceIdType.MESH


def band_table(count, bins, first):
    samples = np.arange(count, dtype=np.int64)
    freqs = first + np.arange(bins, dtype=np.int64)
    phase = samples[:, None] * freqs[None, :] % count
    angle = phase.astype(np.float64) * (2.0 * math.pi / count)
    return np.concatenate([np.cos(angle), -np.sin(angle)], axis=1).astype(ml_dtypes.bfloat16)


def angle_factors(count, bins, first):
    freqs = first + np.arange(bins, dtype=np.int64)
    coarse = np.arange(count // SPLIT, dtype=np.int64)[:, None] * SPLIT * freqs[None, :] % count
    fine = np.arange(SPLIT, dtype=np.int64)[:, None] * freqs[None, :] % count
    out = []
    for phase in (coarse, fine):
        angle = phase.astype(np.float64) * (2.0 * math.pi / count)
        out += [np.cos(angle).astype(np.float32), np.sin(angle).astype(np.float32)]
    return out


def plain_body(traces, valid, src_station):
    w_dev, r_dev, samples = traces.shape
    bins = F
    n_win = lax.axis_size("win")
    f_dev = bins // n_win
    table = jnp.asarray(band_table(samples, bins, samples // 16))
    spectra = jnp.dot(
        traces.reshape(w_dev * r_dev, samples), table, preferred_element_type=jnp.float32
    )
    power = jnp.sum(spectra * spectra, axis=1, keepdims=True) / bins
    keep = jnp.repeat(valid.astype(jnp.float32), r_dev)[:, None]
    white = (spectra * (lax.rsqrt(power + 1e-06) * keep)).astype(jnp.bfloat16)
    white = white.reshape(w_dev * r_dev, 2, n_win, f_dev)
    pieces = jnp.transpose(white, (2, 1, 0, 3))
    got = lax.all_to_all(pieces, "win", 0, 0, tiled=True)
    got = got.reshape(n_win, 2, w_dev, r_dev, f_dev)
    offset = lax.axis_index("rcv") * r_dev
    station_ids = offset + jnp.arange(r_dev, dtype=jnp.int32)
    selector = (src_station[:, None] == station_ids[None, :]).astype(jnp.bfloat16)
    rows = jnp.einsum("sr,gcwrf->gcwsf", selector, got, preferred_element_type=jnp.float32)
    src = lax.psum(rows.astype(jnp.bfloat16), "rcv")
    scale = 1.0 / math.sqrt(w_dev * n_win)
    turned = jnp.stack([got[:, 1], -got[:, 0]], axis=1)
    real = jnp.einsum("gcwsf,gcwrf->srf", src, got, preferred_element_type=jnp.float32)
    imag = jnp.einsum("gcwsf,gcwrf->srf", src, turned, preferred_element_type=jnp.float32)
    return jnp.stack([real, imag], axis=2) * scale


def kernel(
    nw, nz, w_dev, r_dev, bins,
    traces, c1, s1, c0, s0, valid, stations, out,
    tr, table, spec, snd, got, own, pin, sin, pout, sout, self32, srcf, rf,
    tsem, ysend, yrecv, psend, precv, ssend, srecv,
):
    me = lax.axis_index("win")
    z = lax.axis_index("rcv")
    f_dev = bins // nw
    n_src = out.shape[0]
    half = nw // 2
    units = w_dev // MM
    chip = me // half
    core = lax.rem(me, half)
    near, far = chip * half, (1 - chip) * half
    peers = [far + core, far + (1 - core), near + (1 - core)]
    senders = peers
    barrier = pltpu.get_barrier_semaphore()

    def load(w):
        return pltpu.make_async_copy(traces.at[w], tr.at[w], tsem.at[w])

    for w in range(w_dev):
        load(w).start()
    for peer in peers:
        pl.semaphore_signal(barrier, inc=1, device_id={"win": peer}, device_id_type=MESH)

    @pl.when(z > 0)
    def _():
        pl.semaphore_signal(barrier, inc=1, device_id={"rcv": z - 1}, device_id_type=MESH)

    @pl.when(z < nz - 1)
    def _():
        pl.semaphore_signal(barrier, inc=1, device_id={"rcv": z + 1}, device_id_type=MESH)

    @pl.when(z == 0)
    def _():
        pin[...] = jnp.zeros_like(pin)

    @pl.when(z == nz - 1)
    def _():
        sin[...] = jnp.zeros_like(sin)

    def build(a, _):
        ca, sa = c1[pl.ds(a, 1), :], s1[pl.ds(a, 1), :]
        rows = pl.ds(pl.multiple_of(a * SPLIT, SPLIT), SPLIT)
        table[rows, 0:bins] = (ca * c0[...] - sa * s0[...]).astype(jnp.bfloat16)
        table[rows, bins:] = (-(sa * c0[...] + ca * s0[...])).astype(jnp.bfloat16)
        return 0

    lax.fori_loop(0, c1.shape[0], build, 0)
    here = lax.broadcasted_iota(jnp.int32, (1, r_dev), 1) + z * r_dev
    for s in range(n_src):
        self32[s:s + 1, :] = jnp.where(here == stations[s], 1.0, 0.0).astype(jnp.float32)
    out[...] = jnp.zeros_like(out)

    @pl.when((z > 0) & (z < nz - 1))
    def _():
        pl.semaphore_wait(barrier, nw + 1)

    @pl.when((z == 0) | (z == nz - 1))
    def _():
        pl.semaphore_wait(barrier, nw)

    def y_copy(k, w):
        return pltpu.make_async_remote_copy(
            src_ref=snd.at[peers[k], w], dst_ref=got.at[me, w],
            send_sem=ysend.at[k, w], recv_sem=yrecv.at[k, w],
            device_id={"win": peers[k]}, device_id_type=MESH,
        )

    def y_arrival(k, w):
        return pltpu.make_async_remote_copy(
            src_ref=snd.at[peers[k], w], dst_ref=got.at[senders[k], w],
            send_sem=ysend.at[k, w], recv_sem=yrecv.at[k, w],
            device_id={"win": peers[k]}, device_id_type=MESH,
        )

    def transform(t):
        for wl in range(MM):
            load(t * MM + wl).wait()
        x = tr[pl.ds(t * MM, MM)].reshape(MM * r_dev, tr.shape[2])
        for nb in range(2 * bins // 256):
            cols = slice(nb * 256, nb * 256 + 256)
            spec[:, cols] = jnp.dot(x, table[:, cols], preferred_element_type=jnp.float32)
        for wl in range(MM):
            w = t * MM + wl
            rows = slice(wl * r_dev, (wl + 1) * r_dev)
            s = spec[rows, :]
            power = jnp.sum(s * s, axis=1, keepdims=True) / bins
            gain = lax.rsqrt(power + 1e-06) * valid[w].astype(jnp.float32)
            for d in range(nw):
                for c in range(2):
                    lo = c * bins + d * f_dev
                    snd[d, w, c] = (spec[rows, lo:lo + f_dev] * gain).astype(jnp.bfloat16)
            for k in range(nw - 1):
                y_copy(k, w).start()
            got[me, w] = snd[me, w]

    def unit(h, j):
        return (0, pl.ds(j * MM, MM)) if h == 0 else (1, pl.ds(j, 1))

    def sem(h, j):
        return j if h == 0 else units + j

    def right(h, j):
        return pltpu.make_async_remote_copy(
            src_ref=pout.at[unit(h, j)], dst_ref=pin.at[unit(h, j)],
            send_sem=psend.at[sem(h, j)], recv_sem=precv.at[sem(h, j)],
            device_id={"rcv": lax.rem(z + 1, nz)}, device_id_type=MESH,
        )

    def left(h, j):
        return pltpu.make_async_remote_copy(
            src_ref=sout.at[unit(h, j)], dst_ref=sin.at[unit(h, j)],
            send_sem=ssend.at[sem(h, j)], recv_sem=srecv.at[sem(h, j)],
            device_id={"rcv": lax.rem(z + nz - 1, nz)}, device_id_type=MESH,
        )

    def select(h, w):
        pick = self32[...].astype(jnp.bfloat16)
        for gl in range(half):
            for c in range(2):
                own[h, w, gl, c] = jnp.dot(
                    pick, got[(near, far)[h] + gl, w, c], preferred_element_type=jnp.float32
                ).astype(jnp.bfloat16)

    def hops(h, clock, count):
        jr = clock - z
        jl = clock - (nz - 1 - z)

        @pl.when((jr >= 0) & (jr < count))
        def _():
            @pl.when(z > 0)
            def _():
                right(h, jr).wait_recv()

            @pl.when(z < nz - 1)
            def _():
                pout[unit(h, jr)] = own[unit(h, jr)] + pin[unit(h, jr)]
                right(h, jr).start()

        @pl.when((jl >= 0) & (jl < count))
        def _():
            @pl.when(z < nz - 1)
            def _():
                left(h, jl).wait_recv()

            @pl.when(z > 0)
            def _():
                sout[unit(h, jl)] = own[unit(h, jl)] + sin[unit(h, jl)]
                left(h, jl).start()

    def correlate(w):
        for h in range(2):
            for gl in range(half):
                i = h * half + gl
                g = (near, far)[h] + gl
                for c in range(2):
                    srcf[i, c] = (
                        own[h, w, gl, c] + pin[h, w, gl, c] + sin[h, w, gl, c]
                    ).astype(jnp.float32)
                re = got[g, w, 0].astype(jnp.float32)
                im = got[g, w, 1].astype(jnp.float32)
                rf[i, 0, pl.ds(0, r_dev, stride=2), :] = re
                rf[i, 0, pl.ds(1, r_dev, stride=2), :] = im
                rf[i, 1, pl.ds(0, r_dev, stride=2), :] = im
                rf[i, 1, pl.ds(1, r_dev, stride=2), :] = -re

        def accumulate(s, _):
            total = out[s]
            for i in range(nw):
                total = total + srcf[i, 0, pl.ds(s, 1), :] * rf[i, 0]
                total = total + srcf[i, 1, pl.ds(s, 1), :] * rf[i, 1]
            out[s] = total
            return 0

        lax.fori_loop(0, n_src, accumulate, 0)

    def step(it, _):
        @pl.when(it < units)
        def _():
            transform(it)
            for wl in range(MM):
                y_arrival(2, it * MM + wl).wait_recv()
                select(0, it * MM + wl)

        hops(0, it, units)

        @pl.when((it >= LAG) & (it < w_dev + LAG))
        def _():
            y_arrival(0, it - LAG).wait_recv()
            y_arrival(1, it - LAG).wait_recv()
            select(1, it - LAG)

        hops(1, it - LAG, w_dev)

        @pl.when(it >= LAG + nz - 1)
        def _():
            correlate(it - LAG - (nz - 1))

        return 0

    lax.fori_loop(0, w_dev + LAG + nz - 1, step, 0)

    def drain(w, _):
        for k in range(nw - 1):
            y_copy(k, w).wait_send()
        return 0

    lax.fori_loop(0, w_dev, drain, 0)

    for h, count in ((0, units), (1, w_dev)):
        def drain_chain(j, _, h=h):
            @pl.when(z < nz - 1)
            def _():
                right(h, j).wait_send()

            @pl.when(z > 0)
            def _():
                left(h, j).wait_send()

            return 0

        lax.fori_loop(0, count, drain_chain, 0)


def body(traces, valid, src_station):
    w_dev, r_dev, samples = traces.shape
    nw, nz = lax.axis_size("win"), lax.axis_size("rcv")
    f_dev = F // nw
    n_src = src_station.shape[0]
    if nw != 4 or f_dev % 128 or r_dev % 16 or w_dev % MM:
        return plain_body(traces, valid, src_station)
    factors = [jnp.asarray(f) for f in angle_factors(samples, F, samples // 16)]
    vmem = pl.BlockSpec(memory_space=pltpu.VMEM)
    bf16, f32 = jnp.bfloat16, jnp.float32
    spectra = (nw, w_dev, 2, r_dev, f_dev)
    rows = (2, w_dev, nw // 2, 2, n_src, f_dev)
    chain = (w_dev // MM + w_dev,)
    smem = pl.BlockSpec(memory_space=pltpu.SMEM)
    dma = pltpu.SemaphoreType.DMA
    stacks = pl.pallas_call(
        functools.partial(kernel, nw, nz, w_dev, r_dev, F),
        out_shape=jax.ShapeDtypeStruct((n_src, 2 * r_dev, f_dev), f32),
        in_specs=[pl.BlockSpec(memory_space=pltpu.HBM)] + [vmem] * 4 + [smem] * 2,
        out_specs=vmem,
        scratch_shapes=[
            pltpu.VMEM((w_dev, r_dev, samples), bf16),
            pltpu.VMEM((samples, 2 * F), bf16),
            pltpu.VMEM((MM * r_dev, 2 * F), f32),
            pltpu.VMEM(spectra, bf16),
            pltpu.VMEM(spectra, bf16),
        ] + [pltpu.VMEM(rows, bf16)] * 5 + [
            pltpu.VMEM((n_src, r_dev), f32),
            pltpu.VMEM((nw, 2, n_src, f_dev), f32),
            pltpu.VMEM((nw, 2, 2 * r_dev, f_dev), f32),
            dma((w_dev,)), dma((nw - 1, w_dev)), dma((nw - 1, w_dev)),
            dma(chain), dma(chain), dma(chain), dma(chain),
        ],
        compiler_params=pltpu.CompilerParams(
            collective_id=0, has_side_effects=True, vmem_limit_bytes=32 * 1024 * 1024
        ),
    )(traces, *factors, valid, src_station)
    scale = 1.0 / math.sqrt(w_dev * nw)
    return (stacks * scale).reshape(n_src, r_dev, 2, f_dev)


def solution(mesh):
    return jax.shard_map(
        body,
        mesh=mesh,
        in_specs=(P("win", ("groups", "rcv"), None), P(("groups", "win")), P("groups")),
        out_specs=P(None, ("groups", "rcv"), None, "win"),
        check_vma=False,
    )
```

```python
import functools
import math

import jax
import jax.numpy as jnp
import ml_dtypes
import numpy as np
from jax import lax
from jax.experimental import pallas as pl
from jax.experimental.pallas import tpu as pltpu
from jax.sharding import PartitionSpec as P

F = 512
SPLIT = 64
MM = 2
LAG = 1
HOP = 2
GRANT = 48
MESH = pl.DeviceIdType.MESH


def band_table(count, bins, first):
    samples = np.arange(count, dtype=np.int64)
    freqs = first + np.arange(bins, dtype=np.int64)
    phase = samples[:, None] * freqs[None, :] % count
    angle = phase.astype(np.float64) * (2.0 * math.pi / count)
    return np.concatenate([np.cos(angle), -np.sin(angle)], axis=1).astype(ml_dtypes.bfloat16)


def angle_factors(count, bins, first):
    freqs = first + np.arange(bins, dtype=np.int64)
    coarse = np.arange(count // SPLIT, dtype=np.int64)[:, None] * SPLIT * freqs[None, :] % count
    fine = np.arange(SPLIT, dtype=np.int64)[:, None] * freqs[None, :] % count
    out = []
    for phase in (coarse, fine):
        angle = phase.astype(np.float64) * (2.0 * math.pi / count)
        out += [np.cos(angle).astype(np.float32), np.sin(angle).astype(np.float32)]
    return out


def plain_body(traces, valid, src_station):
    w_dev, r_dev, samples = traces.shape
    bins = F
    n_win = lax.axis_size("win")
    f_dev = bins // n_win
    table = jnp.asarray(band_table(samples, bins, samples // 16))
    spectra = jnp.dot(
        traces.reshape(w_dev * r_dev, samples), table, preferred_element_type=jnp.float32
    )
    power = jnp.sum(spectra * spectra, axis=1, keepdims=True) / bins
    keep = jnp.repeat(valid.astype(jnp.float32), r_dev)[:, None]
    white = (spectra * (lax.rsqrt(power + 1e-06) * keep)).astype(jnp.bfloat16)
    white = white.reshape(w_dev * r_dev, 2, n_win, f_dev)
    pieces = jnp.transpose(white, (2, 1, 0, 3))
    got = lax.all_to_all(pieces, "win", 0, 0, tiled=True)
    got = got.reshape(n_win, 2, w_dev, r_dev, f_dev)
    offset = lax.axis_index("rcv") * r_dev
    station_ids = offset + jnp.arange(r_dev, dtype=jnp.int32)
    selector = (src_station[:, None] == station_ids[None, :]).astype(jnp.bfloat16)
    rows = jnp.einsum("sr,gcwrf->gcwsf", selector, got, preferred_element_type=jnp.float32)
    src = lax.psum(rows.astype(jnp.bfloat16), "rcv")
    scale = 1.0 / math.sqrt(w_dev * n_win)
    turned = jnp.stack([got[:, 1], -got[:, 0]], axis=1)
    real = jnp.einsum("gcwsf,gcwrf->srf", src, got, preferred_element_type=jnp.float32)
    imag = jnp.einsum("gcwsf,gcwrf->srf", src, turned, preferred_element_type=jnp.float32)
    return jnp.stack([real, imag], axis=2) * scale


def kernel(
    nw, nz, w_dev, r_dev, bins,
    traces, factors, valid, stations, out,
    tr, table, spec, snd, got, own, pin, sin, pout, sout, self32, srcf, rf,
    tsem, ysend, yrecv, psend, precv, ssend, srecv,
):
    me = lax.axis_index("win")
    z = lax.axis_index("rcv")
    f_dev = bins // nw
    n_src = out.shape[0]
    half = nw // 2
    units = w_dev // MM
    chip = me // half
    core = lax.rem(me, half)
    near, far = chip * half, (1 - chip) * half
    peers = [far + core, far + (1 - core), near + (1 - core)]
    senders = peers
    barrier = pltpu.get_barrier_semaphore()

    def load(w):
        return pltpu.make_async_copy(traces.at[w], tr.at[w], tsem.at[w])

    for w in range(w_dev):
        load(w).start()
    for peer in peers:
        pl.semaphore_signal(barrier, inc=1, device_id={"win": peer}, device_id_type=MESH)

    @pl.when(z > 0)
    def _():
        pl.semaphore_signal(barrier, inc=1, device_id={"rcv": z - 1}, device_id_type=MESH)

    @pl.when(z < nz - 1)
    def _():
        pl.semaphore_signal(barrier, inc=1, device_id={"rcv": z + 1}, device_id_type=MESH)

    @pl.when(z == 0)
    def _():
        pin[...] = jnp.zeros_like(pin)

    @pl.when(z == nz - 1)
    def _():
        sin[...] = jnp.zeros_like(sin)

    coarse = tr.shape[2] // SPLIT
    fine = slice(2 * coarse, 2 * coarse + SPLIT)
    fine_sin = slice(2 * coarse + SPLIT, 2 * coarse + 2 * SPLIT)

    def build(a, _):
        ca, sa = factors[pl.ds(a, 1), :], factors[pl.ds(coarse + a, 1), :]
        c0, s0 = factors[fine, :], factors[fine_sin, :]
        rows = pl.ds(pl.multiple_of(a * SPLIT, SPLIT), SPLIT)
        table[rows, 0:bins] = (ca * c0 - sa * s0).astype(jnp.bfloat16)
        table[rows, bins:] = (-(sa * c0 + ca * s0)).astype(jnp.bfloat16)
        return 0

    lax.fori_loop(0, coarse, build, 0)
    here = lax.broadcasted_iota(jnp.int32, (1, r_dev), 1) + z * r_dev
    for s in range(n_src):
        self32[s:s + 1, :] = jnp.where(here == stations[s], 1.0, 0.0).astype(jnp.float32)
    out[...] = jnp.zeros_like(out)

    @pl.when((z > 0) & (z < nz - 1))
    def _():
        pl.semaphore_wait(barrier, nw + 1)

    @pl.when((z == 0) | (z == nz - 1))
    def _():
        pl.semaphore_wait(barrier, nw)

    def y_copy(k, w):
        return pltpu.make_async_remote_copy(
            src_ref=snd.at[peers[k], w], dst_ref=got.at[me, w],
            send_sem=ysend.at[k, w], recv_sem=yrecv.at[k, w],
            device_id={"win": peers[k]}, device_id_type=MESH,
        )

    def y_arrival(k, w):
        return pltpu.make_async_remote_copy(
            src_ref=snd.at[peers[k], w], dst_ref=got.at[senders[k], w],
            send_sem=ysend.at[k, w], recv_sem=yrecv.at[k, w],
            device_id={"win": peers[k]}, device_id_type=MESH,
        )

    def transform(t):
        for wl in range(MM):
            load(t * MM + wl).wait()
        x = tr[pl.ds(t * MM, MM)].reshape(MM * r_dev, tr.shape[2])
        for nb in range(2 * bins // 256):
            cols = slice(nb * 256, nb * 256 + 256)
            spec[:, cols] = jnp.dot(x, table[:, cols], preferred_element_type=jnp.float32)
        for wl in range(MM):
            w = t * MM + wl
            rows = slice(wl * r_dev, (wl + 1) * r_dev)
            s = spec[rows, :]
            power = jnp.sum(s * s, axis=1, keepdims=True) / bins
            gain = lax.rsqrt(power + 1e-06) * valid[w].astype(jnp.float32)
            for d in range(nw):
                for c in range(2):
                    lo = c * bins + d * f_dev
                    snd[d, w, c] = (spec[rows, lo:lo + f_dev] * gain).astype(jnp.bfloat16)
            for k in range(nw - 1):
                y_copy(k, w).start()
            got[me, w] = snd[me, w]

    def unit(h, j):
        return (0, pl.ds(j * MM, MM)) if h == 0 else (1, pl.ds(j, 1))

    def sem(h, j):
        return j if h == 0 else units + j

    def right(h, j):
        return pltpu.make_async_remote_copy(
            src_ref=pout.at[unit(h, j)], dst_ref=pin.at[unit(h, j)],
            send_sem=psend.at[sem(h, j)], recv_sem=precv.at[sem(h, j)],
            device_id={"rcv": lax.rem(z + 1, nz)}, device_id_type=MESH,
        )

    def left(h, j):
        return pltpu.make_async_remote_copy(
            src_ref=sout.at[unit(h, j)], dst_ref=sin.at[unit(h, j)],
            send_sem=ssend.at[sem(h, j)], recv_sem=srecv.at[sem(h, j)],
            device_id={"rcv": lax.rem(z + nz - 1, nz)}, device_id_type=MESH,
        )

    def select(h, w):
        pick = self32[...].astype(jnp.bfloat16)
        for gl in range(half):
            for c in range(2):
                own[h, w, gl, c] = jnp.dot(
                    pick, got[(near, far)[h] + gl, w, c], preferred_element_type=jnp.float32
                ).astype(jnp.bfloat16)

    def hops(h, clock, count):
        jr = clock - HOP * z
        jl = clock - HOP * (nz - 1 - z)

        @pl.when((jr >= 0) & (jr < count))
        def _():
            @pl.when(z > 0)
            def _():
                right(h, jr).wait_recv()

            @pl.when(z < nz - 1)
            def _():
                pout[unit(h, jr)] = own[unit(h, jr)] + pin[unit(h, jr)]
                right(h, jr).start()

        @pl.when((jl >= 0) & (jl < count))
        def _():
            @pl.when(z < nz - 1)
            def _():
                left(h, jl).wait_recv()

            @pl.when(z > 0)
            def _():
                sout[unit(h, jl)] = own[unit(h, jl)] + sin[unit(h, jl)]
                left(h, jl).start()

    def correlate(w):
        for h in range(2):
            for gl in range(half):
                i = h * half + gl
                g = (near, far)[h] + gl
                for c in range(2):
                    srcf[i, c] = (
                        own[h, w, gl, c] + pin[h, w, gl, c] + sin[h, w, gl, c]
                    ).astype(jnp.float32)
                re = got[g, w, 0].astype(jnp.float32)
                im = got[g, w, 1].astype(jnp.float32)
                rf[i, 0, pl.ds(0, r_dev, stride=2), :] = re
                rf[i, 0, pl.ds(1, r_dev, stride=2), :] = im
                rf[i, 1, pl.ds(0, r_dev, stride=2), :] = im
                rf[i, 1, pl.ds(1, r_dev, stride=2), :] = -re

        def accumulate(q, _):
            for lo in range(0, 2 * r_dev, r_dev):
                rows = slice(lo, lo + r_dev)
                totals = [out[q * 4 + u, rows, :] for u in range(4)]
                for i in range(nw):
                    for c in range(2):
                        other = rf[i, c, rows, :]
                        totals = [
                            total + srcf[i, c, pl.ds(q * 4 + u, 1), :] * other
                            for u, total in enumerate(totals)
                        ]
                for u in range(4):
                    out[q * 4 + u, rows, :] = totals[u]
            return 0

        lax.fori_loop(0, n_src // 4, accumulate, 0)

    def step(it, _):
        @pl.when(it < units)
        def _():
            transform(it)
            for wl in range(MM):
                y_arrival(2, it * MM + wl).wait_recv()
                select(0, it * MM + wl)

        hops(0, it, units)

        @pl.when((it >= LAG) & (it < w_dev + LAG))
        def _():
            y_arrival(0, it - LAG).wait_recv()
            y_arrival(1, it - LAG).wait_recv()
            select(1, it - LAG)

        hops(1, it - LAG, w_dev)

        @pl.when(it >= LAG + HOP * (nz - 1))
        def _():
            correlate(it - LAG - HOP * (nz - 1))

        return 0

    lax.fori_loop(0, w_dev + LAG + HOP * (nz - 1), step, 0)

    def drain(w, _):
        for k in range(nw - 1):
            y_copy(k, w).wait_send()
        return 0

    lax.fori_loop(0, w_dev, drain, 0)

    for h, count in ((0, units), (1, w_dev)):
        def drain_chain(j, _, h=h):
            @pl.when(z < nz - 1)
            def _():
                right(h, j).wait_send()

            @pl.when(z > 0)
            def _():
                left(h, j).wait_send()

            return 0

        lax.fori_loop(0, count, drain_chain, 0)


def body(traces, valid, src_station):
    w_dev, r_dev, samples = traces.shape
    nw, nz = lax.axis_size("win"), lax.axis_size("rcv")
    f_dev = F // nw
    n_src = src_station.shape[0]
    if nw != 4 or f_dev % 128 or r_dev % 16 or w_dev % MM or n_src % 4:
        return plain_body(traces, valid, src_station)
    factors = jnp.asarray(np.concatenate(angle_factors(samples, F, samples // 16)))
    vmem = pl.BlockSpec(memory_space=pltpu.VMEM)
    bf16, f32 = jnp.bfloat16, jnp.float32
    spectra = (nw, w_dev, 2, r_dev, f_dev)
    rows = (2, w_dev, nw // 2, 2, n_src, f_dev)
    chain = (w_dev // MM + w_dev,)
    smem = pl.BlockSpec(memory_space=pltpu.SMEM)
    dma = pltpu.SemaphoreType.DMA
    stacks = pl.pallas_call(
        functools.partial(kernel, nw, nz, w_dev, r_dev, F),
        out_shape=jax.ShapeDtypeStruct((n_src, 2 * r_dev, f_dev), f32),
        in_specs=[pl.BlockSpec(memory_space=pltpu.HBM)] + [vmem] + [smem] * 2,
        out_specs=vmem,
        scratch_shapes=[
            pltpu.VMEM((w_dev, r_dev, samples), bf16),
            pltpu.VMEM((samples, 2 * F), bf16),
            pltpu.VMEM((MM * r_dev, 2 * F), f32),
            pltpu.VMEM(spectra, bf16),
            pltpu.VMEM(spectra, bf16),
        ] + [pltpu.VMEM(rows, bf16)] * 5 + [
            pltpu.VMEM((n_src, r_dev), f32),
            pltpu.VMEM((nw, 2, n_src, f_dev), f32),
            pltpu.VMEM((nw, 2, 2 * r_dev, f_dev), f32),
            dma((w_dev,)), dma((nw - 1, w_dev)), dma((nw - 1, w_dev)),
            dma(chain), dma(chain), dma(chain), dma(chain),
        ],
        compiler_params=pltpu.CompilerParams(
            collective_id=0, has_side_effects=True, vmem_limit_bytes=GRANT * 1024 * 1024
        ),
    )(traces, factors, valid, src_station)
    scale = 1.0 / math.sqrt(w_dev * nw)
    return (stacks * scale).reshape(n_src, r_dev, 2, f_dev)


def solution(mesh):
    return jax.shard_map(
        body,
        mesh=mesh,
        in_specs=(P("win", ("groups", "rcv"), None), P(("groups", "win")), P("groups")),
        out_specs=P(None, ("groups", "rcv"), None, "win"),
        check_vma=False,
    )
```

```python
import functools
import math

import jax
import jax.numpy as jnp
import ml_dtypes
import numpy as np
from jax import lax
from jax.experimental import pallas as pl
from jax.experimental.pallas import tpu as pltpu
from jax.sharding import PartitionSpec as P

F = 512
SPLIT = 64
MM = 2
LAG = 1
HOP = (1, 2)
GRANT = 48
MESH = pl.DeviceIdType.MESH


def band_table(count, bins, first):
    samples = np.arange(count, dtype=np.int64)
    freqs = first + np.arange(bins, dtype=np.int64)
    phase = samples[:, None] * freqs[None, :] % count
    angle = phase.astype(np.float64) * (2.0 * math.pi / count)
    return np.concatenate([np.cos(angle), -np.sin(angle)], axis=1).astype(ml_dtypes.bfloat16)


def angle_factors(count, bins, first):
    freqs = first + np.arange(bins, dtype=np.int64)
    coarse = np.arange(count // SPLIT, dtype=np.int64)[:, None] * SPLIT * freqs[None, :] % count
    fine = np.arange(SPLIT, dtype=np.int64)[:, None] * freqs[None, :] % count
    out = []
    for phase in (coarse, fine):
        angle = phase.astype(np.float64) * (2.0 * math.pi / count)
        out += [np.cos(angle).astype(np.float32), np.sin(angle).astype(np.float32)]
    return out


def plain_body(traces, valid, src_station):
    w_dev, r_dev, samples = traces.shape
    bins = F
    n_win = lax.axis_size("win")
    f_dev = bins // n_win
    table = jnp.asarray(band_table(samples, bins, samples // 16))
    spectra = jnp.dot(
        traces.reshape(w_dev * r_dev, samples), table, preferred_element_type=jnp.float32
    )
    power = jnp.sum(spectra * spectra, axis=1, keepdims=True) / bins
    keep = jnp.repeat(valid.astype(jnp.float32), r_dev)[:, None]
    white = (spectra * (lax.rsqrt(power + 1e-06) * keep)).astype(jnp.bfloat16)
    white = white.reshape(w_dev * r_dev, 2, n_win, f_dev)
    pieces = jnp.transpose(white, (2, 1, 0, 3))
    got = lax.all_to_all(pieces, "win", 0, 0, tiled=True)
    got = got.reshape(n_win, 2, w_dev, r_dev, f_dev)
    offset = lax.axis_index("rcv") * r_dev
    station_ids = offset + jnp.arange(r_dev, dtype=jnp.int32)
    selector = (src_station[:, None] == station_ids[None, :]).astype(jnp.bfloat16)
    rows = jnp.einsum("sr,gcwrf->gcwsf", selector, got, preferred_element_type=jnp.float32)
    src = lax.psum(rows.astype(jnp.bfloat16), "rcv")
    scale = 1.0 / math.sqrt(w_dev * n_win)
    turned = jnp.stack([got[:, 1], -got[:, 0]], axis=1)
    real = jnp.einsum("gcwsf,gcwrf->srf", src, got, preferred_element_type=jnp.float32)
    imag = jnp.einsum("gcwsf,gcwrf->srf", src, turned, preferred_element_type=jnp.float32)
    return jnp.stack([real, imag], axis=2) * scale


def kernel(
    nw, nz, w_dev, r_dev, bins,
    traces, factors, valid, stations, out,
    tr, table, spec, snd, got, own, pin, sin, pout, sout, self32, srcf, rf,
    tsem, ysend, yrecv, psend, precv, ssend, srecv,
):
    me = lax.axis_index("win")
    z = lax.axis_index("rcv")
    f_dev = bins // nw
    n_src = out.shape[0]
    half = nw // 2
    units = w_dev // MM
    chip = me // half
    core = lax.rem(me, half)
    near, far = chip * half, (1 - chip) * half
    peers = [far + core, far + (1 - core), near + (1 - core)]
    senders = peers
    barrier = pltpu.get_barrier_semaphore()

    def load(w):
        return pltpu.make_async_copy(traces.at[w], tr.at[w], tsem.at[w])

    for w in range(w_dev):
        load(w).start()
    for peer in peers:
        pl.semaphore_signal(barrier, inc=1, device_id={"win": peer}, device_id_type=MESH)

    @pl.when(z > 0)
    def _():
        pl.semaphore_signal(barrier, inc=1, device_id={"rcv": z - 1}, device_id_type=MESH)

    @pl.when(z < nz - 1)
    def _():
        pl.semaphore_signal(barrier, inc=1, device_id={"rcv": z + 1}, device_id_type=MESH)

    @pl.when(z == 0)
    def _():
        pin[...] = jnp.zeros_like(pin)

    @pl.when(z == nz - 1)
    def _():
        sin[...] = jnp.zeros_like(sin)

    coarse = tr.shape[2] // SPLIT
    fine = slice(2 * coarse, 2 * coarse + SPLIT)
    fine_sin = slice(2 * coarse + SPLIT, 2 * coarse + 2 * SPLIT)

    def build(a, _):
        ca, sa = factors[pl.ds(a, 1), :], factors[pl.ds(coarse + a, 1), :]
        c0, s0 = factors[fine, :], factors[fine_sin, :]
        rows = pl.ds(pl.multiple_of(a * SPLIT, SPLIT), SPLIT)
        table[rows, 0:bins] = (ca * c0 - sa * s0).astype(jnp.bfloat16)
        table[rows, bins:] = (-(sa * c0 + ca * s0)).astype(jnp.bfloat16)
        return 0

    lax.fori_loop(0, coarse, build, 0)
    here = lax.broadcasted_iota(jnp.int32, (1, r_dev), 1) + z * r_dev
    for s in range(n_src):
        self32[s:s + 1, :] = jnp.where(here == stations[s], 1.0, 0.0).astype(jnp.float32)
    out[...] = jnp.zeros_like(out)

    @pl.when((z > 0) & (z < nz - 1))
    def _():
        pl.semaphore_wait(barrier, nw + 1)

    @pl.when((z == 0) | (z == nz - 1))
    def _():
        pl.semaphore_wait(barrier, nw)

    def y_copy(k, w):
        return pltpu.make_async_remote_copy(
            src_ref=snd.at[peers[k], w], dst_ref=got.at[me, w],
            send_sem=ysend.at[k, w], recv_sem=yrecv.at[k, w],
            device_id={"win": peers[k]}, device_id_type=MESH,
        )

    def y_arrival(k, w):
        return pltpu.make_async_remote_copy(
            src_ref=snd.at[peers[k], w], dst_ref=got.at[senders[k], w],
            send_sem=ysend.at[k, w], recv_sem=yrecv.at[k, w],
            device_id={"win": peers[k]}, device_id_type=MESH,
        )

    def transform(t):
        for wl in range(MM):
            load(t * MM + wl).wait()
        x = tr[pl.ds(t * MM, MM)].reshape(MM * r_dev, tr.shape[2])
        for nb in range(2 * bins // 256):
            cols = slice(nb * 256, nb * 256 + 256)
            spec[:, cols] = jnp.dot(x, table[:, cols], preferred_element_type=jnp.float32)
        for wl in range(MM):
            w = t * MM + wl
            rows = slice(wl * r_dev, (wl + 1) * r_dev)
            s = spec[rows, :]
            power = jnp.sum(s * s, axis=1, keepdims=True) / bins
            gain = lax.rsqrt(power + 1e-06) * valid[w].astype(jnp.float32)
            for d in range(nw):
                for c in range(2):
                    lo = c * bins + d * f_dev
                    snd[d, w, c] = (spec[rows, lo:lo + f_dev] * gain).astype(jnp.bfloat16)
            for k in range(nw - 1):
                y_copy(k, w).start()
            got[me, w] = snd[me, w]

    def unit(h, j):
        return (0, pl.ds(j * MM, MM)) if h == 0 else (1, pl.ds(j, 1))

    def sem(h, j):
        return j if h == 0 else units + j

    def right(h, j):
        return pltpu.make_async_remote_copy(
            src_ref=pout.at[unit(h, j)], dst_ref=pin.at[unit(h, j)],
            send_sem=psend.at[sem(h, j)], recv_sem=precv.at[sem(h, j)],
            device_id={"rcv": lax.rem(z + 1, nz)}, device_id_type=MESH,
        )

    def left(h, j):
        return pltpu.make_async_remote_copy(
            src_ref=sout.at[unit(h, j)], dst_ref=sin.at[unit(h, j)],
            send_sem=ssend.at[sem(h, j)], recv_sem=srecv.at[sem(h, j)],
            device_id={"rcv": lax.rem(z + nz - 1, nz)}, device_id_type=MESH,
        )

    def select(h, w):
        pick = self32[...].astype(jnp.bfloat16)
        for gl in range(half):
            for c in range(2):
                own[h, w, gl, c] = jnp.dot(
                    pick, got[(near, far)[h] + gl, w, c], preferred_element_type=jnp.float32
                ).astype(jnp.bfloat16)

    def hops(h, clock, count):
        jr = clock - HOP[h] * z
        jl = clock - HOP[h] * (nz - 1 - z)

        @pl.when((jr >= 0) & (jr < count))
        def _():
            @pl.when(z > 0)
            def _():
                right(h, jr).wait_recv()

            @pl.when(z < nz - 1)
            def _():
                pout[unit(h, jr)] = own[unit(h, jr)] + pin[unit(h, jr)]
                right(h, jr).start()

        @pl.when((jl >= 0) & (jl < count))
        def _():
            @pl.when(z < nz - 1)
            def _():
                left(h, jl).wait_recv()

            @pl.when(z > 0)
            def _():
                sout[unit(h, jl)] = own[unit(h, jl)] + sin[unit(h, jl)]
                left(h, jl).start()

    def correlate(h, w):
        for gl in range(half):
            i, g = gl, (near, far)[h] + gl
            for c in range(2):
                srcf[i, c] = (
                    own[h, w, gl, c] + pin[h, w, gl, c] + sin[h, w, gl, c]
                ).astype(jnp.float32)
            re = got[g, w, 0].astype(jnp.float32)
            im = got[g, w, 1].astype(jnp.float32)
            rf[i, 0, pl.ds(0, r_dev, stride=2), :] = re
            rf[i, 0, pl.ds(1, r_dev, stride=2), :] = im
            rf[i, 1, pl.ds(0, r_dev, stride=2), :] = im
            rf[i, 1, pl.ds(1, r_dev, stride=2), :] = -re

        def accumulate(q, _):
            for lo in range(0, 2 * r_dev, r_dev):
                rows = slice(lo, lo + r_dev)
                totals = [out[q * 4 + u, rows, :] for u in range(4)]
                for i in range(half):
                    for c in range(2):
                        other = rf[i, c, rows, :]
                        totals = [
                            total + srcf[i, c, pl.ds(q * 4 + u, 1), :] * other
                            for u, total in enumerate(totals)
                        ]
                for u in range(4):
                    out[q * 4 + u, rows, :] = totals[u]
            return 0

        lax.fori_loop(0, n_src // 4, accumulate, 0)

    def step(it, _):
        @pl.when(it < units)
        def _():
            transform(it)
            for wl in range(MM):
                y_arrival(2, it * MM + wl).wait_recv()
                select(0, it * MM + wl)

        hops(0, it, units)

        @pl.when((it >= LAG) & (it < w_dev + LAG))
        def _():
            y_arrival(0, it - LAG).wait_recv()
            y_arrival(1, it - LAG).wait_recv()
            select(1, it - LAG)

        hops(1, it - LAG, w_dev)

        near_unit = it - HOP[0] * (nz - 1)

        @pl.when((near_unit >= 0) & (near_unit < units))
        def _():
            for wl in range(MM):
                correlate(0, near_unit * MM + wl)

        far_window = it - LAG - HOP[1] * (nz - 1)

        @pl.when(far_window >= 0)
        def _():
            correlate(1, far_window)

        return 0

    lax.fori_loop(0, w_dev + LAG + HOP[1] * (nz - 1), step, 0)

    def drain(w, _):
        for k in range(nw - 1):
            y_copy(k, w).wait_send()
        return 0

    lax.fori_loop(0, w_dev, drain, 0)

    for h, count in ((0, units), (1, w_dev)):
        def drain_chain(j, _, h=h):
            @pl.when(z < nz - 1)
            def _():
                right(h, j).wait_send()

            @pl.when(z > 0)
            def _():
                left(h, j).wait_send()

            return 0

        lax.fori_loop(0, count, drain_chain, 0)


def body(traces, valid, src_station):
    w_dev, r_dev, samples = traces.shape
    nw, nz = lax.axis_size("win"), lax.axis_size("rcv")
    f_dev = F // nw
    n_src = src_station.shape[0]
    if nw != 4 or f_dev % 128 or r_dev % 16 or w_dev % MM or n_src % 4:
        return plain_body(traces, valid, src_station)
    factors = jnp.asarray(np.concatenate(angle_factors(samples, F, samples // 16)))
    vmem = pl.BlockSpec(memory_space=pltpu.VMEM)
    bf16, f32 = jnp.bfloat16, jnp.float32
    spectra = (nw, w_dev, 2, r_dev, f_dev)
    rows = (2, w_dev, nw // 2, 2, n_src, f_dev)
    chain = (w_dev // MM + w_dev,)
    smem = pl.BlockSpec(memory_space=pltpu.SMEM)
    dma = pltpu.SemaphoreType.DMA
    stacks = pl.pallas_call(
        functools.partial(kernel, nw, nz, w_dev, r_dev, F),
        out_shape=jax.ShapeDtypeStruct((n_src, 2 * r_dev, f_dev), f32),
        in_specs=[pl.BlockSpec(memory_space=pltpu.HBM)] + [vmem] + [smem] * 2,
        out_specs=vmem,
        scratch_shapes=[
            pltpu.VMEM((w_dev, r_dev, samples), bf16),
            pltpu.VMEM((samples, 2 * F), bf16),
            pltpu.VMEM((MM * r_dev, 2 * F), f32),
            pltpu.VMEM(spectra, bf16),
            pltpu.VMEM(spectra, bf16),
        ] + [pltpu.VMEM(rows, bf16)] * 5 + [
            pltpu.VMEM((n_src, r_dev), f32),
            pltpu.VMEM((nw // 2, 2, n_src, f_dev), f32),
            pltpu.VMEM((nw // 2, 2, 2 * r_dev, f_dev), f32),
            dma((w_dev,)), dma((nw - 1, w_dev)), dma((nw - 1, w_dev)),
            dma(chain), dma(chain), dma(chain), dma(chain),
        ],
        compiler_params=pltpu.CompilerParams(
            collective_id=0, has_side_effects=True, vmem_limit_bytes=GRANT * 1024 * 1024
        ),
    )(traces, factors, valid, src_station)
    scale = 1.0 / math.sqrt(w_dev * nw)
    return (stacks * scale).reshape(n_src, r_dev, 2, f_dev)


def solution(mesh):
    return jax.shard_map(
        body,
        mesh=mesh,
        in_specs=(P("win", ("groups", "rcv"), None), P(("groups", "win")), P("groups")),
        out_specs=P(None, ("groups", "rcv"), None, "win"),
        check_vma=False,
    )
```
